256 devices in a mesh: row: 32 (over y, z), col: 8 (over x, core).
Axes of the slice: x: 4, y: 4, z: 8, core: 2. Of those that a mesh axis runs over, the one named last changes fastest.
Arguments:
- trail_adjoint: float32 [24576, 24576], P('row', 'col'), may hold values from -3 to 3
- panel: float32 [24576, 256], P(('row', 'col')), may hold values from -0.0390625 to 0.0390625
- panel_adjoint: float32 [24576, 256], P(('row', 'col')), may hold values from -6 to 6
- diag_factor: float32 [256, 256], replicated, as said below
- diag_inverse: float32 [256, 256], replicated, as said below
- diag_adjoint: float32 [256, 256], replicated, may hold values from -6 to 6
Outputs:
- panel_grad: float32 [24576, 256], P(('row', 'col'))
- diag_grad: float32 [256, 256], replicated
The draws below stay inside these ranges and needn't reach their ends.
Inputs may be any that keep to these rules, and one draw needn't show every extreme that they name: diag_factor is lower triangular with a diagonal between 1 and 2, and diag_inverse is its inverse. diag_factor is lower triangular with a diagonal between 1 and 2.
All inputs are finite; a program needn't handle non-finite values.
Results may differ from the reference program's by a relative error of at most 0.000057.
Values sent between devices are 32-bit elements; how exact they have to be, the bound alone decides.
A program may use at most 128 MiB of HBM per device.

```python
import math
import jax
import jax.numpy as jnp
from jax import lax

B = 256
M = 24576


def triangle_block(key):
    diag_key = jax.random.fold_in(key, 11)
    off_key = jax.random.fold_in(key, 12)
    diagonal = jnp.exp(jax.random.uniform(diag_key, (B,), jnp.float32) * math.log(2.0))
    off_part = jax.random.normal(off_key, (B, B), jnp.float32) * (0.5 / math.sqrt(B))
    return jnp.tril(off_part, -1) + jnp.diag(diagonal)


def draw_diag_factor(key, part):
    return triangle_block(key)


def draw_diag_inverse(key, part):
    factor = triangle_block(key)
    return jax.scipy.linalg.solve_triangular(factor, jnp.eye(B, dtype=jnp.float32), lower=True)


def level_of(rng, shape, pieces, low, top_value):
    factor_of = 1.0
    for dim, blocks in pieces:
        draws = jax.random.uniform(jax.random.fold_in(jax.random.fold_in(rng, 6), dim), (blocks,), jnp.float32, low / len(pieces), top_value / len(pieces))
        factor_of = factor_of * jnp.repeat(jnp.exp(draws), shape[dim] // blocks).reshape((-1,) + (1,) * (len(shape) - 1 - dim))
    return factor_of


def gaussian(key, dims, scale, bound, cuts=(), kind=jnp.bfloat16):
    array = scale * jax.random.normal(key, dims, jnp.float32)
    if cuts:
        array = array * level_of(key, dims, cuts, -0.22, 0.18)
    return jnp.clip(array, -bound, bound).astype(kind)


def setup_inputs(seed: int = 0) -> dict:
    streams_of = jax.random.split(jax.random.key(seed), 7)
    return {
        "trail_adjoint": gaussian(streams_of[0], (M, M), 0.5, 3.0, ((0, 32), (1, 8)), jnp.float32),
        "panel": gaussian(streams_of[1], (M, B), M ** -0.5, 0.0390625, ((0, 256),), jnp.float32),
        "panel_adjoint": gaussian(streams_of[2], (M, B), 1.0, 6.0, ((0, 256),), jnp.float32),
        "diag_factor": draw_diag_factor(jax.random.fold_in(streams_of[6], 71), 0),
        "diag_inverse": draw_diag_inverse(jax.random.fold_in(streams_of[6], 71), 0),
        "diag_adjoint": gaussian(streams_of[5], (B, B), 1.0, 6.0, (), jnp.float32),
    }


def lower_half(matrix):
    return jnp.tril(matrix) - 0.5 * jnp.diag(jnp.diag(matrix))

def reference(trail_adjoint, panel, panel_adjoint, diag_factor, diag_inverse, diag_adjoint):
    highest = lax.Precision.HIGHEST
    image = jnp.dot(trail_adjoint.astype(jnp.float32), panel.astype(jnp.float32), precision=highest, preferred_element_type=jnp.float32)
    updated = panel_adjoint - 2.0 * image
    panel_grad = jnp.dot(updated.astype(jnp.float32), diag_inverse.astype(jnp.float32), precision=highest, preferred_element_type=jnp.float32)
    gram = jnp.dot(panel_grad.T.astype(jnp.float32), panel.astype(jnp.float32), precision=highest, preferred_element_type=jnp.float32)
    corner = diag_adjoint - gram
    inner = lower_half(jnp.dot(diag_factor.T.astype(jnp.float32), corner.astype(jnp.float32), precision=highest, preferred_element_type=jnp.float32))
    left_part = jnp.dot(diag_inverse.T.astype(jnp.float32), inner.astype(jnp.float32), precision=highest, preferred_element_type=jnp.float32)
    diag_grad = lower_half(jnp.dot(left_part.astype(jnp.float32), diag_inverse.astype(jnp.float32), precision=highest, preferred_element_type=jnp.float32))
    return (panel_grad, diag_grad)
```

```python
import jax
import jax.numpy as jnp
from jax import lax
from jax.experimental import pallas as pl
from jax.experimental.pallas import tpu as pltpu
from jax.sharding import PartitionSpec as P

MESH = pl.DeviceIdType.MESH
F32 = jnp.float32
BF16 = jnp.bfloat16
HIGHEST = lax.Precision.HIGHEST

NX, NY, NZ = 4, 4, 8
ROWS = 96
WIDE = 256
CHUNK = 768
FIRST = 48
SECOND = ROWS - FIRST
CUT = 24


def dot(a, b):
    return jnp.dot(a, b, precision=HIGHEST, preferred_element_type=F32)


def lower_half(matrix):
    i = lax.broadcasted_iota(jnp.int32, matrix.shape, 0)
    j = lax.broadcasted_iota(jnp.int32, matrix.shape, 1)
    return jnp.where(i > j, matrix, jnp.where(i == j, 0.5 * matrix, 0.0))


def kernel(
    trail, panel, panel_adjoint, diag_factor, diag_inverse, diag_adjoint,
    panel_grad, diag_grad,
    raw, high, low, gathered, ring, p_high, p_low, image, parts,
    gram_local, gram_parts, tiles, tile_parts, row_tiles, all_tiles, gram,
    trail_sem,
    s1u_send, s1u_recv, s1z_send, s1z_recv,
    s2z_send, s2z_recv, s2u_send, s2u_recv,
    rs_send, rs_recv, ga_send, ga_recv, gb_send, gb_recv,
    gc_send, gc_recv, gd_send, gd_recv,
):
    r = lax.axis_index("row")
    q = lax.axis_index("col")
    y, z = r // NZ, r % NZ
    x, c = q // 2, q % 2
    half = z // 4

    loads = [
        pltpu.make_async_copy(
            trail.at[:, pl.ds(j * CHUNK, CHUNK)], raw.at[j], trail_sem.at[j]
        )
        for j in range(4)
    ]
    for load in loads:
        load.start()

    def col_peer(dx, dc):
        return ((x + dx) % NX) * 2 + (c + dc) % 2

    barrier = pltpu.get_barrier_semaphore()

    def greet(row, col):
        pl.semaphore_signal(barrier, inc=1, device_id=(row, col), device_id_type=MESH)

    for dx in range(4):
        for dc in range(2):
            if (dx, dc) == (0, 0):
                @pl.when(x != y)
                def _():
                    greet(x * NZ + z, q)
            else:
                greet(x * NZ + z, col_peer(dx, dc))
    for dy in range(4):
        for dz in range(8):
            if (dy, dz) != (0, 0):
                greet(((y + dy) % NY) * NZ + (z + dz) % NZ, q)
    for dx in range(4):
        for dc in range(2):
            if (dx, dc) != (0, 0):
                greet(r, col_peer(dx, dc))

    ring[z] = panel[FIRST:, :]
    image[...] = jnp.zeros_like(image)

    @pl.when(x == y)
    def _():
        pl.semaphore_wait(barrier, 7 + 31 + 7)

    @pl.when(x != y)
    def _():
        pl.semaphore_wait(barrier, 8 + 31 + 7)

    sent = []

    def remote(src, dst, send, recv, row, col):
        return pltpu.make_async_remote_copy(
            src_ref=src, dst_ref=dst, send_sem=send, recv_sem=recv,
            device_id=(row, col), device_id_type=MESH,
        )

    def go(copy):
        copy.start()
        sent.append((None, copy))

    def spread(src, slot, rows, core, send, recv):
        dst = gathered.at[slot, q, rows]
        for dy in (2, 1, 3, 0):
            copy = remote(src, dst, send.at[dy], recv, ((y + dy) % NY) * NZ + z, 2 * y + core)
            if dy:
                go(copy)
            else:
                own = (x == y) & (core == c)

                @pl.when(own)
                def _():
                    pltpu.make_async_copy(src, dst, recv).start()

                @pl.when(jnp.logical_not(own))
                def _():
                    copy.start()

                sent.append((jnp.logical_not(own), copy))

    top, bottom = pl.ds(0, FIRST), pl.ds(FIRST, SECOND)
    up, down = y * NZ + (z + 1) % NZ, y * NZ + (z + 7) % NZ
    towards = (up, down)

    def origin(way, s):
        return (z - s + 8) % NZ if way == 0 else (z + s) % NZ

    def ring_part(o, way, s):
        if s < 4:
            return ring.at[o]
        return ring.at[o, pl.ds(0, CUT)] if way == 0 else ring.at[o, pl.ds(CUT, SECOND - CUT)]

    def bundle_part(o, way, s):
        if s < 4:
            return gathered.at[o % 4, :, top]
        return gathered.at[o % 4, pl.ds(4 * way, 4), top]

    def s2z(way, s):
        ref = ring_part(origin(way, s - 1), way, s)
        return remote(ref, ref, s2z_send.at[way, s - 1], s2z_recv.at[way, s - 1], towards[way], q)

    def s2z_wait(way, s):
        ref = ring_part(origin(way, s), way, s)
        remote(ref, ref, s2z_send.at[way, s - 1], s2z_recv.at[way, s - 1], towards[way], q).wait_recv()

    def s2u(way, s):
        o = origin(way, s)
        spread(ring.at[o], o % 4, bottom, o // 4, s2u_send.at[way, s], s2u_recv.at[o % 4])

    def s1z_start(s):
        for way in range(2):
            o = origin(way, s - 1)
            ref = bundle_part(o, way, s)
            copy = remote(ref, ref, s1z_send.at[way, s - 1], s1z_recv.at[way, s - 1], towards[way], q)
            mine = o // 4 == c

            @pl.when(mine)
            def _():
                copy.start()

            sent.append((mine, copy))

    def s1z_wait(s):
        for way in range(2):
            o = origin(way, s)

            @pl.when(o // 4 == c)
            def _():
                ref = bundle_part(o, way, s)
                remote(
                    ref, ref, s1z_send.at[way, s - 1], s1z_recv.at[way, s - 1], towards[way], q
                ).wait_recv()

    def split_trail(j):
        loads[j].wait()

        @pl.loop(0, CHUNK, step=32)
        def _(i):
            rows = pl.ds(pl.multiple_of(i, 32), 32)
            value = raw[j, rows, :]
            head = value.astype(BF16)
            high[j, rows, :] = head
            low[j, rows, :] = (value - head.astype(F32)).astype(BF16)

    def multiply(o):
        @pl.when(o // 4 == c)
        def _():
            j = o % 4
            pltpu.make_async_copy(
                gathered.at[j, :, bottom], gathered.at[j, :, bottom], s2u_recv.at[j]
            ).wait()
            block = gathered[j].reshape(CHUNK, WIDE)
            head = block.astype(BF16)
            p_high[...] = head
            p_low[...] = (block - head.astype(F32)).astype(BF16)

            @pl.loop(0, CHUNK, step=256)
            def _(i):
                rows = pl.ds(pl.multiple_of(i, 256), 256)
                a, b = high[j, rows, :], low[j, rows, :]
                image[rows, :] += (
                    jnp.dot(a, p_high[...], preferred_element_type=F32)
                    + jnp.dot(a, p_low[...], preferred_element_type=F32)
                    + jnp.dot(b, p_high[...], preferred_element_type=F32)
                )

    spread(panel.at[top], z % 4, top, half, s1u_send, s1u_recv)
    go(s2z(0, 1))
    go(s2z(1, 1))
    s2u(0, 0)
    split_trail(0)

    @pl.when(half == c)
    def _():
        ref = gathered.at[z % 4, :, top]
        pltpu.make_async_copy(ref, ref, s1u_recv).wait()

    s1z_start(1)
    for s in (1, 2, 3):
        for way in range(2):
            s2z_wait(way, s)
            go(s2z(way, s + 1))
            s2u(way, s)
        if s == 1:
            split_trail(1)
        if s == 2:
            s1z_wait(1)
            s1z_start(2)
            split_trail(2)
    for way in range(2):
        s2z_wait(way, 4)
    s2u(0, 4)
    split_trail(3)
    multiply(z)
    s1z_wait(2)
    s1z_start(3)
    multiply(origin(0, 1))
    multiply(origin(1, 1))
    s1z_wait(3)
    s1z_start(4)
    for s in (2, 3):
        multiply(origin(0, s))
        multiply(origin(1, s))
    s1z_wait(4)
    multiply(origin(0, 4))

    peers = [(dx, dc) for dx in (2, 1, 3, 0) for dc in (0, 1) if (dx, dc) != (0, 0)]
    for n, (dx, dc) in enumerate(peers):
        to = col_peer(dx, dc)
        go(remote(
            image.at[pl.ds(pl.multiple_of(to * ROWS, ROWS), ROWS)], parts.at[n],
            rs_send.at[n], rs_recv, r, to,
        ))
    pltpu.make_async_copy(parts, parts, rs_recv).wait()
    total = image[pl.ds(pl.multiple_of(q * ROWS, ROWS), ROWS), :]
    for n in range(7):
        total = total + parts[n]
    updated = panel_adjoint[...] - 2.0 * total
    grad = dot(updated, diag_inverse[...])
    panel_grad[...] = grad
    gram_local[...] = dot(grad.T, panel[...])

    for n, (dx, dc) in enumerate(peers):
        to = col_peer(dx, dc)
        go(remote(
            gram_local.at[pl.ds(pl.multiple_of(to * 32, 32), 32)], gram_parts.at[n],
            ga_send.at[n], ga_recv, r, to,
        ))
    pltpu.make_async_copy(gram_parts, gram_parts, ga_recv).wait()
    slab = gram_local[pl.ds(pl.multiple_of(q * 32, 32), 32), :]
    for n in range(7):
        slab = slab + gram_parts[n]
    for t in range(8):
        tiles[t] = slab[8 * (t // 2) : 8 * (t // 2) + 8, 128 * (t % 2) : 128 * (t % 2) + 128]
    n = 0
    for dz in (4, 3, 5, 2, 6, 1, 7, 0):
        for dy in (2, 1, 3, 0):
            if (dy, dz) != (0, 0):
                to_z = (z + dz) % NZ
                go(remote(
                    tiles.at[to_z], tile_parts.at[r], gb_send.at[n], gb_recv,
                    ((y + dy) % NY) * NZ + to_z, q,
                ))
                n += 1
    tile_parts[r] = tiles[z]
    pltpu.make_async_copy(
        tile_parts.at[pl.ds(0, 31)], tile_parts.at[pl.ds(0, 31)], gb_recv
    ).wait()
    row_tiles[z] = jnp.sum(tile_parts[...], axis=0)
    for n, dz in enumerate((4, 3, 5, 2, 6, 1, 7)):
        go(remote(
            row_tiles.at[z], row_tiles.at[z], gc_send.at[n], gc_recv, y * NZ + (z + dz) % NZ, q,
        ))
    pltpu.make_async_copy(row_tiles.at[pl.ds(0, 7)], row_tiles.at[pl.ds(0, 7)], gc_recv).wait()
    for n, (dx, dc) in enumerate(peers):
        go(remote(row_tiles, all_tiles.at[q], gd_send.at[n], gd_recv, r, col_peer(dx, dc)))
    all_tiles[q] = row_tiles[...]
    pltpu.make_async_copy(
        all_tiles.at[pl.ds(0, 7)], all_tiles.at[pl.ds(0, 7)], gd_recv
    ).wait()
    for k in range(8):
        for t in range(8):
            i, j = 32 * k + 8 * (t // 2), 128 * (t % 2)
            gram[i : i + 8, j : j + 128] = all_tiles[k, t]

    corner = diag_adjoint[...] - gram[...]
    inner = lower_half(dot(diag_factor[...].T, corner))
    left = dot(diag_inverse[...].T, inner)
    diag_grad[...] = lower_half(dot(left, diag_inverse[...]))

    for condition, copy in sent:
        if condition is None:
            copy.wait_send()
        else:
            pl.when(condition)(copy.wait_send)


def on_device(trail_adjoint, panel, panel_adjoint, diag_factor, diag_inverse, diag_adjoint):
    vmem = pl.BlockSpec(memory_space=pltpu.VMEM)
    dma = pltpu.SemaphoreType.DMA
    return pl.pallas_call(
        kernel,
        out_shape=(
            jax.ShapeDtypeStruct((ROWS, WIDE), F32),
            jax.ShapeDtypeStruct((WIDE, WIDE), F32),
        ),
        in_specs=[pl.BlockSpec(memory_space=pl.ANY)] + [vmem] * 5,
        out_specs=(vmem, vmem),
        scratch_shapes=[
            pltpu.VMEM((4, CHUNK, CHUNK), F32),
            pltpu.VMEM((4, CHUNK, CHUNK), BF16),
            pltpu.VMEM((4, CHUNK, CHUNK), BF16),
            pltpu.VMEM((4, 8, ROWS, WIDE), F32),
            pltpu.VMEM((8, SECOND, WIDE), F32),
            pltpu.VMEM((CHUNK, WIDE), BF16),
            pltpu.VMEM((CHUNK, WIDE), BF16),
            pltpu.VMEM((CHUNK, WIDE), F32),
            pltpu.VMEM((7, ROWS, WIDE), F32),
            pltpu.VMEM((WIDE, WIDE), F32),
            pltpu.VMEM((7, 32, WIDE), F32),
            pltpu.VMEM((8, 8, 128), F32),
            pltpu.VMEM((32, 8, 128), F32),
            pltpu.VMEM((8, 8, 128), F32),
            pltpu.VMEM((8, 8, 8, 128), F32),
            pltpu.VMEM((WIDE, WIDE), F32),
            dma((4,)),
            dma((4,)), dma, dma((2, 4)), dma((2, 4)),
            dma((2, 4)), dma((2, 4)), dma((2, 5, 4)), dma((4,)),
            dma((7,)), dma, dma((7,)), dma, dma((31,)), dma,
            dma((7,)), dma, dma((7,)), dma,
        ],
        compiler_params=pltpu.CompilerParams(
            collective_id=0, has_side_effects=True, vmem_limit_bytes=56 * 1024 * 1024
        ),
    )(trail_adjoint, panel, panel_adjoint, diag_factor, diag_inverse, diag_adjoint)


def solution(mesh):
    in_specs = (P("row", "col"), P(("row", "col"), None), P(("row", "col"), None), P(), P(), P())
    out_specs = (P(("row", "col"), None), P())
    return jax.shard_map(
        on_device, mesh=mesh, in_specs=in_specs, out_specs=out_specs, check_vma=False
    )
```

```python
import jax
import jax.numpy as jnp
from jax import lax
from jax.experimental import pallas as pl
from jax.experimental.pallas import tpu as pltpu
from jax.sharding import PartitionSpec as P

MESH = pl.DeviceIdType.MESH
F32 = jnp.float32
BF16 = jnp.bfloat16
HIGHEST = lax.Precision.HIGHEST

NX, NY, NZ = 4, 4, 8
ROWS = 96
WIDE = 256
CHUNK = 768
FIRST = 40
SECOND = ROWS - FIRST


def dot(a, b):
    return jnp.dot(a, b, precision=HIGHEST, preferred_element_type=F32)


def lower_half(matrix):
    i = lax.broadcasted_iota(jnp.int32, matrix.shape, 0)
    j = lax.broadcasted_iota(jnp.int32, matrix.shape, 1)
    return jnp.where(i > j, matrix, jnp.where(i == j, 0.5 * matrix, 0.0))


def kernel(
    trail, panel, panel_adjoint, diag_factor, diag_inverse, diag_adjoint,
    panel_grad, diag_grad,
    raw, high, low, gathered, stage, p_high, p_low, image,
    row_panel, turned_high, turned_low, early, chain, base, inverse_t,
    gram_local, gram_parts, slab, slab_parts, gram,
    core_parts, x_source, x_parts,
    trail_sem,
    s1y_send, s1y_recv, s1x_send, s1u_recv, s1z_send, s1z_recv,
    s2r_send, s2r_recv, s2z_send, s2z_recv, s2y_send, s2y_recv,
    rp_send, rp_recv, rc_send, rc_recv, rx_send, rx_recv,
    ga_send, ga_recv, gb_send, gb_recv, gc_send, gc_recv,
):
    r = lax.axis_index("row")
    q = lax.axis_index("col")
    y, z = r // NZ, r % NZ
    x, c = q // 2, q % 2
    half = z // 4

    loads = [
        pltpu.make_async_copy(
            trail.at[:, pl.ds(j * CHUNK, CHUNK)], raw.at[j], trail_sem.at[j]
        )
        for j in range(4)
    ]
    for load in loads:
        load.start()

    def col_peer(dx, dc):
        return ((x + dx) % NX) * 2 + (c + dc) % 2

    plane = [
        (dy, dx, dc)
        for dy in (2, 1, 3, 0)
        for dx in (2, 1, 3, 0)
        for dc in (0, 1)
        if (dy, dx, dc) != (0, 0, 0)
    ]
    row_peers = [(dx, dc) for dy, dx, dc in plane if dy == 0]
    depth = (4, 3, 5, 2, 6, 1, 7)

    def plane_peer(dy, dx, dc):
        return ((y + dy) % NY) * NZ + z, col_peer(dx, dc)

    barrier = pltpu.get_barrier_semaphore()

    def greet(row, col):
        pl.semaphore_signal(barrier, inc=1, device_id=(row, col), device_id_type=MESH)

    for peer in plane:
        greet(*plane_peer(*peer))
    for dz in depth:
        greet(y * NZ + (z + dz) % NZ, q)

    sent = []

    def remote(src, dst, send, recv, row, col):
        return pltpu.make_async_remote_copy(
            src_ref=src, dst_ref=dst, send_sem=send, recv_sem=recv,
            device_id=(row, col), device_id_type=MESH,
        )

    def go(copy):
        copy.start()
        sent.append((None, copy))

    def landed(ref, recv):
        pltpu.make_async_copy(ref, ref, recv).wait()

    def one_or_local(copy, own, src, dst, recv):
        @pl.when(own)
        def _():
            pltpu.make_async_copy(src, dst, recv).start()

        @pl.when(jnp.logical_not(own))
        def _():
            copy.start()

        sent.append((jnp.logical_not(own), copy))

    top, bottom = pl.ds(0, FIRST), pl.ds(FIRST, SECOND)
    towards = (y * NZ + (z + 1) % NZ, y * NZ + (z + 7) % NZ)

    def origin(way, s):
        return (z - s + 8) % NZ if way == 0 else (z + s) % NZ

    def top_copy(o, way, s, part):
        ref = gathered.at[o % 4, pl.ds(2 * part, 2), top]
        return remote(
            ref, ref, s1z_send.at[way, s - 1, part], s1z_recv.at[way, s - 1, part], towards[way], q
        )

    def bottom_copy(o, way, s):
        items = pl.ds(2 * y, 2) if s < 4 else pl.ds(2 * y + way, 1)
        ref = gathered.at[o % 4, items, bottom]
        return remote(ref, ref, s2z_send.at[way, s - 1], s2z_recv.at[way, s - 1], towards[way], q)

    def carried(way, s, part):
        return s < 4 or part // 2 == way

    def top_start(s, part):
        for way in range(2):
            if carried(way, s, part):
                o = origin(way, s - 1)
                copy = top_copy(o, way, s, part)
                pl.when(o // 4 == c)(copy.start)
                sent.append((o // 4 == c, copy))

    def top_wait(s, part):
        for way in range(2):
            if carried(way, s, part):
                o = origin(way, s)
                pl.when(o // 4 == c)(top_copy(o, way, s, part).wait_recv)

    def top_step(s, *parts):
        for part in parts:
            top_wait(s, part)
            top_start(s + 1, part)

    def bottom_start(s):
        for way in range(2):
            o = origin(way, s - 1)
            copy = bottom_copy(o, way, s)
            pl.when(o // 4 == c)(copy.start)
            sent.append((o // 4 == c, copy))

    def bottom_wait(s):
        for way in range(2):
            o = origin(way, s)
            pl.when(o // 4 == c)(bottom_copy(o, way, s).wait_recv)

    def bottom_step(s):
        bottom_wait(s)
        bottom_start(s + 1)
        s2y(0, s)
        s2y(1, s)

    def s1x(a, src, n):
        dst = gathered.at[z % 4, q, top]
        copy = remote(src, dst, s1x_send.at[n], s1u_recv, r, 2 * a + half)
        one_or_local(copy, (x == a) & (half == c), src, dst, s1u_recv)

    def s2y(way, s):
        o = origin(way, s)
        mine = o // 4 == c
        ref = gathered.at[o % 4, pl.ds(2 * y, 2), bottom]
        for n, dy in enumerate((2, 1, 3)):
            copy = remote(
                ref, ref, s2y_send.at[way, s, n], s2y_recv.at[o % 4],
                ((y + dy) % NY) * NZ + z, q,
            )
            pl.when(mine)(copy.start)
            sent.append((mine, copy))

    def split_trail(j):
        loads[j].wait()

        @pl.loop(0, CHUNK, step=32)
        def _(i):
            rows = pl.ds(pl.multiple_of(i, 32), 32)
            value = raw[j, rows, :]
            head = value.astype(BF16)
            high[j, rows, :] = head
            low[j, rows, :] = (value - head.astype(F32)).astype(BF16)

    def multiply(o):
        @pl.when(o // 4 == c)
        def _():
            j = o % 4
            landed(gathered.at[j, pl.ds(0, 6), bottom], s2y_recv.at[j])
            block = gathered[j].reshape(CHUNK, WIDE)
            head = block.astype(BF16)
            p_high[...] = head
            p_low[...] = (block - head.astype(F32)).astype(BF16)

            @pl.loop(0, CHUNK, step=256)
            def _(i):
                rows = pl.ds(pl.multiple_of(i, 256), 256)
                a, b = high[j, rows, :], low[j, rows, :]
                image[rows, :] += (
                    jnp.dot(a, p_high[...], preferred_element_type=F32)
                    + jnp.dot(a, p_low[...], preferred_element_type=F32)
                    + jnp.dot(b, p_high[...], preferred_element_type=F32)
                )

    image[...] = jnp.zeros_like(image)
    row_panel[q] = panel[...]
    inverse_t[...] = diag_inverse[...].T
    factor_t = diag_factor[...].T
    chain[...] = dot(factor_t, inverse_t[...])
    base[...] = dot(factor_t, diag_adjoint[...])
    early[...] = dot(panel[...].T, panel_adjoint[...])
    for j in range(4):
        split_trail(j)
    pl.semaphore_wait(barrier, len(plane) + len(depth))

    for n, dy in enumerate((2, 1, 3)):
        go(remote(
            panel.at[top], stage.at[3 - n], s1y_send.at[n], s1y_recv.at[3 - n],
            ((y + dy) % NY) * NZ + z, q,
        ))
    s2r_dst = gathered.at[z % 4, q, bottom]
    s2r = remote(panel.at[bottom], s2r_dst, s2r_send, s2r_recv, x * NZ + z, 2 * y + half)
    one_or_local(s2r, (x == y) & (half == c), panel.at[bottom], s2r_dst, s2r_recv)
    s1x(y, panel.at[top], 0)
    for n, dy in ((1, 1), (2, 3), (0, 2)):
        landed(stage.at[3 - n], s1y_recv.at[3 - n])
        s1x((y - dy + NY) % NY, stage.at[3 - n], 3 - n)

    @pl.when(half == c)
    def _():
        landed(gathered.at[z % 4, pl.ds(0, 2), bottom], s2r_recv)

    bottom_start(1)
    s2y(0, 0)
    for n, (dx, dc) in enumerate(row_peers):
        go(remote(panel, row_panel.at[q], rp_send.at[n], rp_recv, r, col_peer(dx, dc)))

    @pl.when(half == c)
    def _():
        landed(gathered.at[z % 4, :, top], s1u_recv)

    for part in range(4):
        top_start(1, part)
    bottom_step(1)
    top_step(1, 0, 1)
    bottom_step(2)
    top_step(1, 2, 3)
    multiply(z)
    top_step(2, 0, 1)
    bottom_step(3)
    top_step(2, 2, 3)
    multiply(origin(0, 1))
    multiply(origin(1, 1))
    top_wait(3, 0)
    top_start(4, 0)
    top_wait(3, 1)
    top_start(4, 1)
    top_wait(3, 2)
    top_start(4, 2)
    top_wait(3, 3)
    top_start(4, 3)
    bottom_wait(4)
    s2y(0, 4)
    landed(row_panel.at[pl.ds(0, 7)], rp_recv)
    turned = row_panel[...].reshape(CHUNK, WIDE).T
    turned_head = turned.astype(BF16)
    turned_high[...] = turned_head
    turned_low[...] = (turned - turned_head.astype(F32)).astype(BF16)
    for s in (2, 3):
        multiply(origin(0, s))
        multiply(origin(1, s))
    for part in range(4):
        top_wait(4, part)
    multiply(origin(0, 4))

    for n in range(4):
        block = pl.ds(pl.multiple_of((2 * n + 1 - c) * ROWS, ROWS), ROWS)
        go(remote(image.at[block], core_parts.at[n], rc_send.at[n], rc_recv, r, col_peer(0, 1)))

    value = image[...]
    head = value.astype(BF16)
    tail = (value - head.astype(F32)).astype(BF16)
    gram_local[...] = early[...] - 2.0 * (
        jnp.dot(turned_high[...], head, preferred_element_type=F32)
        + jnp.dot(turned_high[...], tail, preferred_element_type=F32)
        + jnp.dot(turned_low[...], head, preferred_element_type=F32)
    )
    me = 8 * y + q
    for n, peer in enumerate(plane):
        row, col = plane_peer(*peer)
        to = 8 * (row // NZ) + col
        go(remote(
            gram_local.at[pl.ds(pl.multiple_of(to * 8, 8), 8)], gram_parts.at[me],
            ga_send.at[n], ga_recv, row, col,
        ))
    gram_parts[me] = gram_local[pl.ds(pl.multiple_of(me * 8, 8), 8), :]
    landed(core_parts, rc_recv)
    for n in range(4):
        block = pl.ds(pl.multiple_of((2 * n + c) * ROWS, ROWS), ROWS)
        x_source[n] = image[block, :] + core_parts[n]
    landed(gram_parts.at[pl.ds(0, 31)], ga_recv)
    slab[...] = jnp.sum(gram_parts[...], axis=0)
    for n, dz in enumerate(depth):
        go(remote(
            slab, slab_parts.at[z], gb_send.at[n], gb_recv, y * NZ + (z + dz) % NZ, q,
        ))
    slab_parts[z] = slab[...]
    for n, dx in enumerate((2, 1, 3)):
        to = (x + dx) % NX
        go(remote(x_source.at[to], x_parts.at[n], rx_send.at[n], rx_recv, r, 2 * to + c))
    landed(slab_parts.at[pl.ds(0, 7)], gb_recv)
    mine = pl.ds(pl.multiple_of(me * 8, 8), 8)
    gram[mine, :] = jnp.sum(slab_parts[...], axis=0)
    for n, peer in enumerate(plane):
        go(remote(gram.at[mine], gram.at[mine], gc_send.at[n], gc_recv, *plane_peer(*peer)))

    landed(x_parts, rx_recv)
    total = x_source[x] + x_parts[0] + x_parts[1] + x_parts[2]
    panel_grad[...] = dot(panel_adjoint[...] - 2.0 * total, diag_inverse[...])

    landed(gram.at[pl.ds(0, 31 * 8)], gc_recv)
    inner = lower_half(
        base[...]
        - lax.dot_general(
            chain[...], gram[...], (((1,), (1,)), ((), ())),
            precision=HIGHEST, preferred_element_type=F32,
        )
    )
    left = dot(inverse_t[...], inner)
    diag_grad[...] = lower_half(dot(left, diag_inverse[...]))

    for condition, copy in sent:
        if condition is None:
            copy.wait_send()
        else:
            pl.when(condition)(copy.wait_send)


def on_device(trail_adjoint, panel, panel_adjoint, diag_factor, diag_inverse, diag_adjoint):
    vmem = pl.BlockSpec(memory_space=pltpu.VMEM)
    dma = pltpu.SemaphoreType.DMA
    return pl.pallas_call(
        kernel,
        out_shape=(
            jax.ShapeDtypeStruct((ROWS, WIDE), F32),
            jax.ShapeDtypeStruct((WIDE, WIDE), F32),
        ),
        in_specs=[pl.BlockSpec(memory_space=pl.ANY)] + [vmem] * 5,
        out_specs=(vmem, vmem),
        scratch_shapes=[
            pltpu.VMEM((4, CHUNK, CHUNK), F32),
            pltpu.VMEM((4, CHUNK, CHUNK), BF16),
            pltpu.VMEM((4, CHUNK, CHUNK), BF16),
            pltpu.VMEM((4, 8, ROWS, WIDE), F32),
            pltpu.VMEM((4, FIRST, WIDE), F32),
            pltpu.VMEM((CHUNK, WIDE), BF16),
            pltpu.VMEM((CHUNK, WIDE), BF16),
            pltpu.VMEM((CHUNK, WIDE), F32),
            pltpu.VMEM((8, ROWS, WIDE), F32),
            pltpu.VMEM((WIDE, CHUNK), BF16),
            pltpu.VMEM((WIDE, CHUNK), BF16),
            pltpu.VMEM((WIDE, WIDE), F32),
            pltpu.VMEM((WIDE, WIDE), F32),
            pltpu.VMEM((WIDE, WIDE), F32),
            pltpu.VMEM((WIDE, WIDE), F32),
            pltpu.VMEM((WIDE, WIDE), F32),
            pltpu.VMEM((32, 8, WIDE), F32),
            pltpu.VMEM((8, WIDE), F32),
            pltpu.VMEM((8, 8, WIDE), F32),
            pltpu.VMEM((WIDE, WIDE), F32),
            pltpu.VMEM((4, ROWS, WIDE), F32),
            pltpu.VMEM((4, ROWS, WIDE), F32),
            pltpu.VMEM((3, ROWS, WIDE), F32),
            dma((4,)),
            dma((3,)), dma((4,)), dma((4,)), dma, dma((2, 4, 4)), dma((2, 4, 4)),
            dma, dma, dma((2, 4)), dma((2, 4)), dma((2, 5, 3)), dma((4,)),
            dma((7,)), dma, dma((4,)), dma, dma((3,)), dma,
            dma((31,)), dma, dma((7,)), dma, dma((31,)), dma,
        ],
        compiler_params=pltpu.CompilerParams(
            collective_id=0, has_side_effects=True, vmem_limit_bytes=56 * 1024 * 1024
        ),
    )(trail_adjoint, panel, panel_adjoint, diag_factor, diag_inverse, diag_adjoint)


def solution(mesh):
    in_specs = (P("row", "col"), P(("row", "col"), None), P(("row", "col"), None), P(), P(), P())
    out_specs = (P(("row", "col"), None), P())
    return jax.shard_map(
        on_device, mesh=mesh, in_specs=in_specs, out_specs=out_specs, check_vma=False
    )
```

```python
import jax
import jax.numpy as jnp
from jax import lax
from jax.experimental import pallas as pl
from jax.experimental.pallas import tpu as pltpu
from jax.sharding import PartitionSpec as P

MESH = pl.DeviceIdType.MESH
F32 = jnp.float32
BF16 = jnp.bfloat16
HIGHEST = lax.Precision.HIGHEST

NX, NY, NZ = 4, 4, 8
ROWS = 96
WIDE = 256
CHUNK = 768
CUT = 24
FIRST = 48
SECOND = ROWS - FIRST


def dot(a, b):
    return jnp.dot(a, b, precision=HIGHEST, preferred_element_type=F32)


def lower_half(matrix):
    i = lax.broadcasted_iota(jnp.int32, matrix.shape, 0)
    j = lax.broadcasted_iota(jnp.int32, matrix.shape, 1)
    return jnp.where(i > j, matrix, jnp.where(i == j, 0.5 * matrix, 0.0))


def kernel(
    trail, panel_in, panel_adjoint_in, diag_factor_in, diag_inverse_in, diag_adjoint_in,
    panel_grad, diag_grad,
    panel, panel_adjoint, diag_factor, diag_inverse, diag_adjoint,
    raw, high, low, gathered, ring, lines, stage, p_high, p_low, image,
    row_panel, turned_high, turned_low, early, chain, base, inverse_t,
    gram_local, gram_parts, slab, slab_parts, gram,
    core_parts, x_source, x_parts,
    z_known, plane_known, input_sem, trail_sem,
    s1y_send, s1y_recv, s1x_send, s1u_recv, s1z_send, s1z_recv,
    s2z_send, s2z_recv, s2y_send, s2y_recv, s2x_send, s2x_recv,
    rp_send, rp_recv, rf_send, rf_recv, rc_send, rc_recv, rx_send, rx_recv,
    ga_send, ga_recv, gb_send, gb_recv, gc_send, gc_recv,
):
    r = lax.axis_index("row")
    q = lax.axis_index("col")
    y, z = r // NZ, r % NZ
    x, c = q // 2, q % 2
    half = z // 4

    def col_peer(dx, dc):
        return ((x + dx) % NX) * 2 + (c + dc) % 2

    plane = [
        (dy, dx, dc)
        for dy in (2, 1, 3, 0)
        for dx in (2, 1, 3, 0)
        for dc in (0, 1)
        if (dy, dx, dc) != (0, 0, 0)
    ]
    row_peers = [(dx, dc) for dy, dx, dc in plane if dy == 0]
    depth = (4, 3, 5, 2, 6, 1, 7)

    def plane_peer(dy, dx, dc):
        return ((y + dy) % NY) * NZ + z, col_peer(dx, dc)

    barrier = pltpu.get_barrier_semaphore()

    def greet(row, col):
        pl.semaphore_signal(barrier, inc=1, device_id=(row, col), device_id_type=MESH)

    towards = (y * NZ + (z + 1) % NZ, y * NZ + (z + 7) % NZ)
    across = [((y + dy) % NY) * NZ + z for dy in (2, 1, 3)]
    for row in across:
        greet(row, q)
    for dx, dc in row_peers:
        greet(r, col_peer(dx, dc))
    for row in towards:
        greet(row, q)

    def tell(sem, rows):
        for row in rows:
            pl.semaphore_signal(sem, inc=1, device_id=(row, q), device_id_type=MESH)

    small = [
        pltpu.make_async_copy(src, dst, input_sem.at[n])
        for n, (src, dst) in enumerate((
            (panel_in, panel), (diag_factor_in, diag_factor), (diag_inverse_in, diag_inverse),
            (diag_adjoint_in, diag_adjoint), (panel_adjoint_in, panel_adjoint),
        ))
    ]
    for load in small:
        load.start()
    loads = [
        pltpu.make_async_copy(
            trail.at[:, pl.ds(j * CHUNK, CHUNK)], raw.at[j], trail_sem.at[j]
        )
        for j in range(4)
    ]
    for load in loads:
        load.start()

    sent = []

    def remote(src, dst, send, recv, row, col):
        return pltpu.make_async_remote_copy(
            src_ref=src, dst_ref=dst, send_sem=send, recv_sem=recv,
            device_id=(row, col), device_id_type=MESH,
        )

    def go(copy):
        copy.start()
        sent.append((None, copy))

    def landed(ref, recv):
        pltpu.make_async_copy(ref, ref, recv).wait()

    def one_or_local(copy, own, src, dst, recv):
        @pl.when(own)
        def _():
            pltpu.make_async_copy(src, dst, recv).start()

        @pl.when(jnp.logical_not(own))
        def _():
            copy.start()

        sent.append((jnp.logical_not(own), copy))

    events_of = ((0, 0), (0, 1), (1, 1), (0, 2), (1, 2), (0, 3), (1, 3), (0, 4))
    top, bottom = pl.ds(0, FIRST), pl.ds(FIRST, SECOND)

    def origin(way, s):
        return (z - s + 8) % NZ if way == 0 else (z + s) % NZ

    def top_copy(o, way, s, part):
        ref = gathered.at[o % 4, pl.ds(2 * ((x + part) % NX), 2), top]
        return remote(
            ref, ref, s1z_send.at[way, s - 1, part], s1z_recv.at[way, s - 1, part], towards[way], q
        )

    def bottom_copy(o, way, s):
        ref = ring.at[o]
        if s == 4:
            ref = ring.at[o, pl.ds(0, CUT)] if way == 0 else ring.at[o, pl.ds(CUT, SECOND - CUT)]
        return remote(ref, ref, s2z_send.at[way, s - 1], s2z_recv.at[way, s - 1], towards[way], q)

    def carried(way, s, part):
        return s < 4 or part // 2 == way

    def top_start(s, part):
        for way in range(2):
            if carried(way, s, part):
                o = origin(way, s - 1)
                copy = top_copy(o, way, s, part)
                pl.when(o // 4 == c)(copy.start)
                sent.append((o // 4 == c, copy))

    def top_wait(s, part):
        for way in range(2):
            if carried(way, s, part):
                o = origin(way, s)
                pl.when(o // 4 == c)(top_copy(o, way, s, part).wait_recv)

    def top_step(s, *parts):
        for part in parts:
            top_wait(s, part)
            top_start(s + 1, part)

    def bottom_start(s):
        for way in range(2):
            go(bottom_copy(origin(way, s - 1), way, s))

    def bottom_wait(s):
        for way in range(2):
            bottom_copy(origin(way, s), way, s).wait_recv()

    def s1x(a, src, n):
        dst = gathered.at[z % 4, q, top]
        copy = remote(src, dst, s1x_send.at[n], s1u_recv.at[x], r, 2 * a + half)
        one_or_local(copy, (x == a) & (half == c), src, dst, s1u_recv.at[x])

    def s2x(e, o, a, src, n):
        dst = gathered.at[o % 4, q, bottom]
        copy = remote(src, dst, s2x_send.at[e, n], s2x_recv.at[o % 4], r, 2 * a + o // 4)
        one_or_local(copy, (x == a) & (o // 4 == c), src, dst, s2x_recv.at[o % 4])

    def s2_out(*events):
        for e in events:
            o = origin(*events_of[e])
            for n, dy in enumerate((2, 1, 3)):
                go(remote(
                    ring.at[o], lines.at[y, o], s2y_send.at[e, n], s2y_recv.at[e, n],
                    ((y + dy) % NY) * NZ + z, q,
                ))
            s2x(e, o, y, ring.at[o], 3)

    def s2_across(*events):
        for e in events:
            o = origin(*events_of[e])
            for n, dy in ((1, 1), (2, 3), (0, 2)):
                a = (y - dy + NY) % NY
                landed(lines.at[a, o], s2y_recv.at[e, n])
                s2x(e, o, a, lines.at[a, o], n)

    def split_trail(j):
        loads[j].wait()

        @pl.loop(0, CHUNK, step=32)
        def _(i):
            rows = pl.ds(pl.multiple_of(i, 32), 32)
            value = raw[j, rows, :]
            head = value.astype(BF16)
            high[j, rows, :] = head
            low[j, rows, :] = (value - head.astype(F32)).astype(BF16)

    def multiply(way, s):
        o = origin(way, s)

        @pl.when(o // 4 == c)
        def _():
            j = o % 4
            landed(gathered.at[j, :, bottom], s2x_recv.at[j])
            block = gathered[j].reshape(CHUNK, WIDE)
            head = block.astype(BF16)
            p_high[...] = head
            p_low[...] = (block - head.astype(F32)).astype(BF16)

            image[...] += (
                jnp.dot(high[j], p_high[...], preferred_element_type=F32)
                + jnp.dot(high[j], p_low[...], preferred_element_type=F32)
                + jnp.dot(low[j], p_high[...], preferred_element_type=F32)
            )

    image[...] = jnp.zeros_like(image)
    for load in small:
        load.wait()
    row_panel[q] = panel[...]
    ring[z] = panel[FIRST:, :]
    split_trail(0)
    split_trail(1)
    pl.semaphore_wait(barrier, 3 + 7 + 2)
    tell(z_known.at[0], towards)
    tell(plane_known, across)

    for n, dy in enumerate((2, 1, 3)):
        go(remote(
            panel.at[top], stage.at[3 - n], s1y_send.at[n], s1y_recv.at[3 - n],
            ((y + dy) % NY) * NZ + z, q,
        ))
    bottom_start(1)
    for n, (dx, dc) in enumerate(((2, 0), (1, 0), (3, 0), (0, 1))):
        go(remote(panel, row_panel.at[q], rp_send.at[n], rp_recv.at[n], r, col_peer(dx, dc)))
    s2_out(0)
    s1x(y, panel.at[top], 0)
    split_trail(2)
    for n, dy in ((1, 1), (2, 3), (0, 2)):
        landed(stage.at[3 - n], s1y_recv.at[3 - n])
        s1x((y - dy + NY) % NY, stage.at[3 - n], 3 - n)

    def top_root(part):
        @pl.when(half == c)
        def _():
            landed(gathered.at[z % 4, pl.ds(0, 2), top], s1u_recv.at[(x + part) % NX])

        top_start(1, part)

    bottom_wait(1)
    bottom_start(2)
    s2_out(1, 2)
    s2_across(0)
    top_root(0)
    bottom_wait(2)
    bottom_start(3)
    pl.semaphore_wait(z_known.at[0], 2)
    tell(z_known.at[1], towards)
    s2_out(3, 4)
    top_root(1)
    top_root(3)
    split_trail(3)
    s2_across(1, 2)
    top_root(2)
    for n, dx in ((1, 1), (2, 3), (0, 2)):
        ref = row_panel.at[2 * ((x - dx + NX) % NX) + c]
        landed(ref, rp_recv.at[n])
        go(remote(ref, ref, rf_send.at[n], rf_recv, r, col_peer(0, 1)))
    landed(row_panel.at[0], rp_recv.at[3])
    bottom_wait(3)
    bottom_start(4)
    pl.semaphore_wait(z_known.at[1], 2)
    tell(z_known.at[2], towards)
    s2_out(5, 6)
    top_step(1, 0, 1)
    s2_across(3, 4)
    top_step(1, 3, 2)
    landed(row_panel.at[pl.ds(0, 3)], rf_recv)
    turned = row_panel[...].reshape(CHUNK, WIDE).T
    turned_head = turned.astype(BF16)
    turned_high[...] = turned_head
    turned_low[...] = (turned - turned_head.astype(F32)).astype(BF16)
    inverse_t[...] = diag_inverse[...].T
    factor_t = diag_factor[...].T
    chain[...] = dot(factor_t, inverse_t[...])
    bottom_wait(4)
    s2_out(7)
    pl.semaphore_wait(z_known.at[2], 2)
    pl.semaphore_wait(plane_known, 3)
    top_step(2, 0, 1)
    s2_across(5, 6)
    base[...] = dot(diag_factor[...].T, diag_adjoint[...])
    early[...] = dot(panel[...].T, panel_adjoint[...])
    top_step(2, 3, 2)
    s2_across(7)
    multiply(0, 0)
    multiply(0, 1)
    multiply(1, 1)
    top_step(3, 0, 1)
    multiply(0, 2)
    multiply(1, 2)
    top_step(3, 3, 2)
    multiply(0, 3)
    multiply(1, 3)
    for part in range(4):
        top_wait(4, part)
    multiply(0, 4)

    for n in range(4):
        block = pl.ds(pl.multiple_of((2 * n + 1 - c) * ROWS, ROWS), ROWS)
        go(remote(image.at[block], core_parts.at[n], rc_send.at[n], rc_recv, r, col_peer(0, 1)))

    value = image[...]
    head = value.astype(BF16)
    tail = (value - head.astype(F32)).astype(BF16)
    gram_local[...] = early[...] - 2.0 * (
        jnp.dot(turned_high[...], head, preferred_element_type=F32)
        + jnp.dot(turned_high[...], tail, preferred_element_type=F32)
        + jnp.dot(turned_low[...], head, preferred_element_type=F32)
    )
    me = 8 * y + q
    for n, peer in enumerate(plane):
        row, col = plane_peer(*peer)
        to = 8 * (row // NZ) + col
        go(remote(
            gram_local.at[pl.ds(pl.multiple_of(to * 8, 8), 8)], gram_parts.at[me],
            ga_send.at[n], ga_recv, row, col,
        ))
    gram_parts[me] = gram_local[pl.ds(pl.multiple_of(me * 8, 8), 8), :]
    landed(core_parts, rc_recv)
    for n in range(4):
        block = pl.ds(pl.multiple_of((2 * n + c) * ROWS, ROWS), ROWS)
        x_source[n] = image[block, :] + core_parts[n]
    landed(gram_parts.at[pl.ds(0, 31)], ga_recv)
    slab[...] = jnp.sum(gram_parts[...], axis=0)
    for n, dz in enumerate(depth):
        go(remote(
            slab, slab_parts.at[z], gb_send.at[n], gb_recv, y * NZ + (z + dz) % NZ, q,
        ))
    slab_parts[z] = slab[...]
    for n, dx in enumerate((2, 1, 3)):
        to = (x + dx) % NX
        go(remote(x_source.at[to], x_parts.at[n], rx_send.at[n], rx_recv, r, 2 * to + c))
    landed(slab_parts.at[pl.ds(0, 7)], gb_recv)
    mine = pl.ds(pl.multiple_of(me * 8, 8), 8)
    gram[mine, :] = jnp.sum(slab_parts[...], axis=0)
    for n, peer in enumerate(plane):
        go(remote(gram.at[mine], gram.at[mine], gc_send.at[n], gc_recv, *plane_peer(*peer)))

    landed(x_parts, rx_recv)
    total = x_source[x] + x_parts[0] + x_parts[1] + x_parts[2]
    panel_grad[...] = dot(panel_adjoint[...] - 2.0 * total, diag_inverse[...])

    landed(gram.at[pl.ds(0, 31 * 8)], gc_recv)
    inner = lower_half(
        base[...]
        - lax.dot_general(
            chain[...], gram[...], (((1,), (1,)), ((), ())),
            precision=HIGHEST, preferred_element_type=F32,
        )
    )
    left = dot(inverse_t[...], inner)
    diag_grad[...] = lower_half(dot(left, diag_inverse[...]))

    for condition, copy in sent:
        if condition is None:
            copy.wait_send()
        else:
            pl.when(condition)(copy.wait_send)


def on_device(trail_adjoint, panel, panel_adjoint, diag_factor, diag_inverse, diag_adjoint):
    vmem = pl.BlockSpec(memory_space=pltpu.VMEM)
    dma = pltpu.SemaphoreType.DMA
    return pl.pallas_call(
        kernel,
        out_shape=(
            jax.ShapeDtypeStruct((ROWS, WIDE), F32),
            jax.ShapeDtypeStruct((WIDE, WIDE), F32),
        ),
        in_specs=[pl.BlockSpec(memory_space=pltpu.HBM)] * 6,
        out_specs=(vmem, vmem),
        scratch_shapes=[
            pltpu.VMEM((ROWS, WIDE), F32),
            pltpu.VMEM((ROWS, WIDE), F32),
            pltpu.VMEM((WIDE, WIDE), F32),
            pltpu.VMEM((WIDE, WIDE), F32),
            pltpu.VMEM((WIDE, WIDE), F32),
            pltpu.VMEM((4, CHUNK, CHUNK), F32),
            pltpu.VMEM((4, CHUNK, CHUNK), BF16),
            pltpu.VMEM((4, CHUNK, CHUNK), BF16),
            pltpu.VMEM((4, 8, ROWS, WIDE), F32),
            pltpu.VMEM((8, SECOND, WIDE), F32),
            pltpu.VMEM((4, 8, SECOND, WIDE), F32),
            pltpu.VMEM((4, FIRST, WIDE), F32),
            pltpu.VMEM((CHUNK, WIDE), BF16),
            pltpu.VMEM((CHUNK, WIDE), BF16),
            pltpu.VMEM((CHUNK, WIDE), F32),
            pltpu.VMEM((8, ROWS, WIDE), F32),
            pltpu.VMEM((WIDE, CHUNK), BF16),
            pltpu.VMEM((WIDE, CHUNK), BF16),
            pltpu.VMEM((WIDE, WIDE), F32),
            pltpu.VMEM((WIDE, WIDE), F32),
            pltpu.VMEM((WIDE, WIDE), F32),
            pltpu.VMEM((WIDE, WIDE), F32),
            pltpu.VMEM((WIDE, WIDE), F32),
            pltpu.VMEM((32, 8, WIDE), F32),
            pltpu.VMEM((8, WIDE), F32),
            pltpu.VMEM((8, 8, WIDE), F32),
            pltpu.VMEM((WIDE, WIDE), F32),
            pltpu.VMEM((4, ROWS, WIDE), F32),
            pltpu.VMEM((4, ROWS, WIDE), F32),
            pltpu.VMEM((3, ROWS, WIDE), F32),
            pltpu.SemaphoreType.REGULAR((3,)), pltpu.SemaphoreType.REGULAR,
            dma((5,)), dma((4,)),
            dma((3,)), dma((4,)), dma((4,)), dma((4,)), dma((2, 4, 4)), dma((2, 4, 4)),
            dma((2, 4)), dma((2, 4)), dma((8, 3)), dma((8, 3)), dma((8, 4)), dma((4,)),
            dma((4,)), dma((4,)), dma((3,)), dma, dma((4,)), dma, dma((3,)), dma,
            dma((31,)), dma, dma((7,)), dma, dma((31,)), dma,
        ],
        compiler_params=pltpu.CompilerParams(
            collective_id=0, has_side_effects=True, vmem_limit_bytes=56 * 1024 * 1024
        ),
    )(trail_adjoint, panel, panel_adjoint, diag_factor, diag_inverse, diag_adjoint)


def solution(mesh):
    in_specs = (P("row", "col"), P(("row", "col"), None), P(("row", "col"), None), P(), P(), P())
    out_specs = (P(("row", "col"), None), P())
    return jax.shard_map(
        on_device, mesh=mesh, in_specs=in_specs, out_specs=out_specs, check_vma=False
    )
```

```python
import jax
import jax.numpy as jnp
from jax import lax
from jax.experimental import pallas as pl
from jax.experimental.pallas import tpu as pltpu
from jax.sharding import PartitionSpec as P

MESH = pl.DeviceIdType.MESH
F32 = jnp.float32
BF16 = jnp.bfloat16
HIGHEST = lax.Precision.HIGHEST

NX, NY, NZ = 4, 4, 8
ROWS = 96
WIDE = 256
CHUNK = 768
CUT = 24
FIRST = 48
SECOND = ROWS - FIRST


def dot(a, b):
    return jnp.dot(a, b, precision=HIGHEST, preferred_element_type=F32)


def lower_half(matrix):
    i = lax.broadcasted_iota(jnp.int32, matrix.shape, 0)
    j = lax.broadcasted_iota(jnp.int32, matrix.shape, 1)
    return jnp.where(i > j, matrix, jnp.where(i == j, 0.5 * matrix, 0.0))


def kernel(
    trail, panel_in, panel_adjoint_in, diag_factor_in, diag_inverse_in, diag_adjoint_in,
    panel_grad, diag_grad,
    panel, panel_adjoint, diag_factor, diag_inverse, diag_adjoint,
    raw, high, low, gathered, ring, lines, stage, p_high, p_low, image,
    row_panel, turned_high, turned_low, early, chain, base, inverse_t,
    gram_local, gram_parts, slab, slab_parts, gram,
    core_parts, x_source, x_parts,
    z_known, plane_known, input_sem, trail_sem,
    s1y_send, s1y_recv, s1x_send, s1u_recv, s1z_send, s1z_recv,
    s2z_send, s2z_recv, s2y_send, s2y_recv, s2x_send, s2x_recv,
    rp_send, rp_recv, rf_send, rf_recv, rc_send, rc_recv, rx_send, rx_recv,
    ga_send, ga_recv, gb_send, gb_recv, gc_send, gc_recv,
):
    r = lax.axis_index("row")
    q = lax.axis_index("col")
    y, z = r // NZ, r % NZ
    x, c = q // 2, q % 2
    half = z // 4

    def col_peer(dx, dc):
        return ((x + dx) % NX) * 2 + (c + dc) % 2

    plane = [
        (dy, dx, dc)
        for dy in (2, 1, 3, 0)
        for dx in (2, 1, 3, 0)
        for dc in (0, 1)
        if (dy, dx, dc) != (0, 0, 0)
    ]
    row_peers = [(dx, dc) for dy, dx, dc in plane if dy == 0]
    depth = (4, 3, 5, 2, 6, 1, 7)

    def plane_peer(dy, dx, dc):
        return ((y + dy) % NY) * NZ + z, col_peer(dx, dc)

    barrier = pltpu.get_barrier_semaphore()

    def greet(row, col):
        pl.semaphore_signal(barrier, inc=1, device_id=(row, col), device_id_type=MESH)

    towards = (y * NZ + (z + 1) % NZ, y * NZ + (z + 7) % NZ)
    across = [((y + dy) % NY) * NZ + z for dy in (2, 1, 3)]
    for row in across:
        greet(row, q)
    for dx, dc in row_peers:
        greet(r, col_peer(dx, dc))
    for row in towards:
        greet(row, q)

    def tell(sem, rows):
        for row in rows:
            pl.semaphore_signal(sem, inc=1, device_id=(row, q), device_id_type=MESH)

    small = [
        pltpu.make_async_copy(src, dst, input_sem.at[n])
        for n, (src, dst) in enumerate((
            (panel_in, panel), (diag_factor_in, diag_factor), (diag_inverse_in, diag_inverse),
            (diag_adjoint_in, diag_adjoint), (panel_adjoint_in, panel_adjoint),
        ))
    ]
    for load in small:
        load.start()
    loads = [
        pltpu.make_async_copy(
            trail.at[:, pl.ds(j * CHUNK, CHUNK)], raw.at[j], trail_sem.at[j]
        )
        for j in range(4)
    ]
    for load in loads:
        load.start()

    sent = []

    def remote(src, dst, send, recv, row, col):
        return pltpu.make_async_remote_copy(
            src_ref=src, dst_ref=dst, send_sem=send, recv_sem=recv,
            device_id=(row, col), device_id_type=MESH,
        )

    def go(copy):
        copy.start()
        sent.append((None, copy))

    def landed(ref, recv):
        pltpu.make_async_copy(ref, ref, recv).wait()

    def one_or_local(copy, own, src, dst, recv):
        @pl.when(own)
        def _():
            pltpu.make_async_copy(src, dst, recv).start()

        @pl.when(jnp.logical_not(own))
        def _():
            copy.start()

        sent.append((jnp.logical_not(own), copy))

    events_of = ((0, 0), (0, 1), (1, 1), (0, 2), (1, 2), (0, 3), (1, 3), (0, 4))
    top, bottom = pl.ds(0, FIRST), pl.ds(FIRST, SECOND)

    def origin(way, s):
        return (z - s + 8) % NZ if way == 0 else (z + s) % NZ

    def top_copy(o, way, s, part):
        ref = gathered.at[o % 4, pl.ds(2 * ((x + part) % NX), 2), top]
        return remote(
            ref, ref, s1z_send.at[way, s - 1, part], s1z_recv.at[way, s - 1, part], towards[way], q
        )

    def bottom_copy(o, way, s):
        ref = ring.at[o]
        if s == 4:
            ref = ring.at[o, pl.ds(0, CUT)] if way == 0 else ring.at[o, pl.ds(CUT, SECOND - CUT)]
        return remote(ref, ref, s2z_send.at[way, s - 1], s2z_recv.at[way, s - 1], towards[way], q)

    def carried(way, s, part):
        return s < 4 or part // 2 == way

    def top_start(s, part):
        for way in range(2):
            if carried(way, s, part):
                o = origin(way, s - 1)
                copy = top_copy(o, way, s, part)
                pl.when(o // 4 == c)(copy.start)
                sent.append((o // 4 == c, copy))

    def top_wait(s, part):
        for way in range(2):
            if carried(way, s, part):
                o = origin(way, s)
                pl.when(o // 4 == c)(top_copy(o, way, s, part).wait_recv)

    def top_step(s, *parts):
        for part in parts:
            top_wait(s, part)
            top_start(s + 1, part)

    def bottom_start(s):
        for way in range(2):
            go(bottom_copy(origin(way, s - 1), way, s))

    def bottom_wait(s):
        for way in range(2):
            bottom_copy(origin(way, s), way, s).wait_recv()

    def s1x(a, src, n):
        dst = gathered.at[z % 4, q, top]
        copy = remote(src, dst, s1x_send.at[n], s1u_recv.at[x], r, 2 * a + half)
        one_or_local(copy, (x == a) & (half == c), src, dst, s1u_recv.at[x])

    def s2x(e, o, a, src, n):
        dst = gathered.at[o % 4, q, bottom]
        copy = remote(src, dst, s2x_send.at[e, n], s2x_recv.at[o % 4], r, 2 * a + o // 4)
        one_or_local(copy, (x == a) & (o // 4 == c), src, dst, s2x_recv.at[o % 4])

    def s2_out(*events):
        for e in events:
            o = origin(*events_of[e])
            for n, dy in enumerate((2, 1, 3)):
                go(remote(
                    ring.at[o], lines.at[y, o], s2y_send.at[e, n], s2y_recv.at[e, n],
                    ((y + dy) % NY) * NZ + z, q,
                ))
            s2x(e, o, y, ring.at[o], 3)

    def s2_across(*events):
        for e in events:
            o = origin(*events_of[e])
            for n, dy in ((1, 1), (2, 3), (0, 2)):
                a = (y - dy + NY) % NY
                landed(lines.at[a, o], s2y_recv.at[e, n])
                s2x(e, o, a, lines.at[a, o], n)

    def split_trail(j):
        loads[j].wait()

        @pl.loop(0, CHUNK, step=32)
        def _(i):
            rows = pl.ds(pl.multiple_of(i, 32), 32)
            value = raw[j, rows, :]
            head = value.astype(BF16)
            high[j, rows, :] = head
            low[j, rows, :] = (value - head.astype(F32)).astype(BF16)

    def multiply(way, s):
        o = origin(way, s)

        @pl.when(o // 4 == c)
        def _():
            j = o % 4
            landed(gathered.at[j, :, bottom], s2x_recv.at[j])
            block = gathered[j].reshape(CHUNK, WIDE)
            head = block.astype(BF16)
            p_high[...] = head
            p_low[...] = (block - head.astype(F32)).astype(BF16)

            image[...] += (
                jnp.dot(high[j], p_high[...], preferred_element_type=F32)
                + jnp.dot(high[j], p_low[...], preferred_element_type=F32)
                + jnp.dot(low[j], p_high[...], preferred_element_type=F32)
            )

    image[...] = jnp.zeros_like(image)
    for load in small:
        load.wait()
    row_panel[q] = panel[...]
    ring[z] = panel[FIRST:, :]
    split_trail(0)
    split_trail(1)
    pl.semaphore_wait(barrier, 3 + 7 + 2)
    tell(z_known.at[0], towards)
    tell(plane_known, across)

    for n, dy in enumerate((2, 1, 3)):
        go(remote(
            panel.at[top], stage.at[3 - n], s1y_send.at[n], s1y_recv.at[3 - n],
            ((y + dy) % NY) * NZ + z, q,
        ))
    bottom_start(1)
    for n, (dx, dc) in enumerate(((2, 0), (1, 0), (3, 0), (0, 1))):
        go(remote(panel, row_panel.at[q], rp_send.at[n], rp_recv.at[n], r, col_peer(dx, dc)))
    s2_out(0)
    s1x(y, panel.at[top], 0)
    split_trail(2)
    for n, dy in ((1, 1), (2, 3), (0, 2)):
        landed(stage.at[3 - n], s1y_recv.at[3 - n])
        s1x((y - dy + NY) % NY, stage.at[3 - n], 3 - n)

    def top_root(part):
        @pl.when(half == c)
        def _():
            landed(gathered.at[z % 4, pl.ds(0, 2), top], s1u_recv.at[(x + part) % NX])

        top_start(1, part)

    bottom_wait(1)
    bottom_start(2)
    s2_out(1, 2)
    s2_across(0)
    top_root(0)
    bottom_wait(2)
    bottom_start(3)
    pl.semaphore_wait(z_known.at[0], 2)
    tell(z_known.at[1], towards)
    s2_out(3, 4)
    top_root(1)
    top_root(3)
    split_trail(3)
    s2_across(1, 2)
    top_root(2)
    for n, dx in ((1, 1), (2, 3), (0, 2)):
        ref = row_panel.at[2 * ((x - dx + NX) % NX) + c]
        landed(ref, rp_recv.at[n])
        go(remote(ref, ref, rf_send.at[n], rf_recv, r, col_peer(0, 1)))
    landed(row_panel.at[0], rp_recv.at[3])
    bottom_wait(3)
    bottom_start(4)
    pl.semaphore_wait(z_known.at[1], 2)
    tell(z_known.at[2], towards)
    s2_out(5, 6)
    top_step(1, 0, 1)
    s2_across(3, 4)
    top_step(1, 3, 2)
    landed(row_panel.at[pl.ds(0, 3)], rf_recv)
    turned = row_panel[...].reshape(CHUNK, WIDE).T
    turned_head = turned.astype(BF16)
    turned_high[...] = turned_head
    turned_low[...] = (turned - turned_head.astype(F32)).astype(BF16)
    inverse_t[...] = diag_inverse[...].T
    factor_t = diag_factor[...].T
    chain[...] = dot(factor_t, inverse_t[...])
    bottom_wait(4)
    s2_out(7)
    pl.semaphore_wait(z_known.at[2], 2)
    pl.semaphore_wait(plane_known, 3)
    top_step(2, 0, 1)
    s2_across(5, 6)
    base[...] = dot(diag_factor[...].T, diag_adjoint[...])
    early[...] = dot(panel[...].T, panel_adjoint[...])
    top_step(2, 3, 2)
    s2_across(7)
    multiply(0, 0)
    multiply(0, 1)
    multiply(1, 1)
    top_step(3, 0, 1)
    multiply(0, 2)
    multiply(1, 2)
    top_step(3, 3, 2)
    multiply(0, 3)
    multiply(1, 3)
    for part in range(4):
        top_wait(4, part)
    multiply(0, 4)

    for n in range(4):
        block = pl.ds(pl.multiple_of((2 * n + 1 - c) * ROWS, ROWS), ROWS)
        go(remote(image.at[block], core_parts.at[n], rc_send.at[n], rc_recv, r, col_peer(0, 1)))

    value = image[...]
    head = value.astype(BF16)
    tail = (value - head.astype(F32)).astype(BF16)
    gram_local[...] = early[...] - 2.0 * (
        jnp.dot(turned_high[...], head, preferred_element_type=F32)
        + jnp.dot(turned_high[...], tail, preferred_element_type=F32)
        + jnp.dot(turned_low[...], head, preferred_element_type=F32)
    )
    me = 8 * y + q
    for n, peer in enumerate(plane):
        row, col = plane_peer(*peer)
        to = 8 * (row // NZ) + col
        go(remote(
            gram_local.at[pl.ds(pl.multiple_of(to * 8, 8), 8)], gram_parts.at[me],
            ga_send.at[n], ga_recv, row, col,
        ))
    gram_parts[me] = gram_local[pl.ds(pl.multiple_of(me * 8, 8), 8), :]
    landed(core_parts, rc_recv)
    for n in range(4):
        block = pl.ds(pl.multiple_of((2 * n + c) * ROWS, ROWS), ROWS)
        x_source[n] = image[block, :] + core_parts[n]
    landed(gram_parts.at[pl.ds(0, 31)], ga_recv)
    slab[...] = jnp.sum(gram_parts[...], axis=0)
    for n, dz in enumerate(depth):
        go(remote(
            slab, slab_parts.at[z], gb_send.at[n], gb_recv, y * NZ + (z + dz) % NZ, q,
        ))
    slab_parts[z] = slab[...]
    for n, dx in enumerate((2, 1, 3)):
        to = (x + dx) % NX
        go(remote(x_source.at[to], x_parts.at[n], rx_send.at[n], rx_recv, r, 2 * to + c))
    landed(slab_parts.at[pl.ds(0, 7)], gb_recv)
    mine = pl.ds(pl.multiple_of(me * 8, 8), 8)
    gram[mine, :] = jnp.sum(slab_parts[...], axis=0)
    for n, peer in enumerate(plane):
        go(remote(gram.at[mine], gram.at[mine], gc_send.at[n], gc_recv, *plane_peer(*peer)))

    landed(x_parts, rx_recv)
    total = x_source[x] + x_parts[0] + x_parts[1] + x_parts[2]
    panel_grad[...] = dot(panel_adjoint[...] - 2.0 * total, diag_inverse[...])

    landed(gram.at[pl.ds(0, 31 * 8)], gc_recv)
    inner = lower_half(
        base[...]
        - lax.dot_general(
            chain[...], gram[...], (((1,), (1,)), ((), ())),
            precision=HIGHEST, preferred_element_type=F32,
        )
    )
    left = dot(inverse_t[...], inner)
    diag_grad[...] = lower_half(dot(left, diag_inverse[...]))

    for condition, copy in sent:
        if condition is None:
            copy.wait_send()
        else:
            pl.when(condition)(copy.wait_send)


def hand_over(grad, diag, grad_out, diag_out, grad_held, diag_held, sem):
    ways = ((diag, diag_held, diag_out), (grad, grad_held, grad_out))
    into = [pltpu.make_async_copy(src, held, sem.at[0, n]) for n, (src, held, _) in enumerate(ways)]
    out = [pltpu.make_async_copy(held, dst, sem.at[1, n]) for n, (_, held, dst) in enumerate(ways)]
    for copy in into:
        copy.start()
    for landing, leaving in zip(into, out):
        landing.wait()
        leaving.start()
    for copy in out:
        copy.wait()


def on_device(trail_adjoint, panel, panel_adjoint, diag_factor, diag_inverse, diag_adjoint):
    vmem = pl.BlockSpec(memory_space=pltpu.VMEM)
    dma = pltpu.SemaphoreType.DMA
    results = pl.pallas_call(
        kernel,
        out_shape=(
            jax.ShapeDtypeStruct((ROWS, WIDE), F32),
            jax.ShapeDtypeStruct((WIDE, WIDE), F32),
        ),
        in_specs=[pl.BlockSpec(memory_space=pltpu.HBM)] * 6,
        out_specs=(vmem, vmem),
        scratch_shapes=[
            pltpu.VMEM((ROWS, WIDE), F32),
            pltpu.VMEM((ROWS, WIDE), F32),
            pltpu.VMEM((WIDE, WIDE), F32),
            pltpu.VMEM((WIDE, WIDE), F32),
            pltpu.VMEM((WIDE, WIDE), F32),
            pltpu.VMEM((4, CHUNK, CHUNK), F32),
            pltpu.VMEM((4, CHUNK, CHUNK), BF16),
            pltpu.VMEM((4, CHUNK, CHUNK), BF16),
            pltpu.VMEM((4, 8, ROWS, WIDE), F32),
            pltpu.VMEM((8, SECOND, WIDE), F32),
            pltpu.VMEM((4, 8, SECOND, WIDE), F32),
            pltpu.VMEM((4, FIRST, WIDE), F32),
            pltpu.VMEM((CHUNK, WIDE), BF16),
            pltpu.VMEM((CHUNK, WIDE), BF16),
            pltpu.VMEM((CHUNK, WIDE), F32),
            pltpu.VMEM((8, ROWS, WIDE), F32),
            pltpu.VMEM((WIDE, CHUNK), BF16),
            pltpu.VMEM((WIDE, CHUNK), BF16),
            pltpu.VMEM((WIDE, WIDE), F32),
            pltpu.VMEM((WIDE, WIDE), F32),
            pltpu.VMEM((WIDE, WIDE), F32),
            pltpu.VMEM((WIDE, WIDE), F32),
            pltpu.VMEM((WIDE, WIDE), F32),
            pltpu.VMEM((32, 8, WIDE), F32),
            pltpu.VMEM((8, WIDE), F32),
            pltpu.VMEM((8, 8, WIDE), F32),
            pltpu.VMEM((WIDE, WIDE), F32),
            pltpu.VMEM((4, ROWS, WIDE), F32),
            pltpu.VMEM((4, ROWS, WIDE), F32),
            pltpu.VMEM((3, ROWS, WIDE), F32),
            pltpu.SemaphoreType.REGULAR((3,)), pltpu.SemaphoreType.REGULAR,
            dma((5,)), dma((4,)),
            dma((3,)), dma((4,)), dma((4,)), dma((4,)), dma((2, 4, 4)), dma((2, 4, 4)),
            dma((2, 4)), dma((2, 4)), dma((8, 3)), dma((8, 3)), dma((8, 4)), dma((4,)),
            dma((4,)), dma((4,)), dma((3,)), dma, dma((4,)), dma, dma((3,)), dma,
            dma((31,)), dma, dma((7,)), dma, dma((31,)), dma,
        ],
        compiler_params=pltpu.CompilerParams(
            collective_id=0, has_side_effects=True, vmem_limit_bytes=56 * 1024 * 1024
        ),
    )(trail_adjoint, panel, panel_adjoint, diag_factor, diag_inverse, diag_adjoint)
    anywhere = pl.BlockSpec(memory_space=pl.ANY)
    return pl.pallas_call(
        hand_over,
        out_shape=(
            jax.ShapeDtypeStruct((ROWS, WIDE), F32),
            jax.ShapeDtypeStruct((WIDE, WIDE), F32),
        ),
        in_specs=[anywhere] * 2,
        out_specs=(anywhere,) * 2,
        scratch_shapes=[pltpu.VMEM((ROWS, WIDE), F32), pltpu.VMEM((WIDE, WIDE), F32), dma((2, 2))],
        compiler_params=pltpu.CompilerParams(vmem_limit_bytes=56 * 1024 * 1024),
    )(*results)


def solution(mesh):
    in_specs = (P("row", "col"), P(("row", "col"), None), P(("row", "col"), None), P(), P(), P())
    out_specs = (P(("row", "col"), None), P())
    return jax.shard_map(
        on_device, mesh=mesh, in_specs=in_specs, out_specs=out_specs, check_vma=False
    )
```
